32 devices in a mesh: leaf: 8 (over z, y), hand: 4 (over x, core).
Axes of the slice: x: 2, y: 2, z: 4, core: 2. Of those that a mesh axis runs over, the one named last changes fastest.
Arguments:
- opp_range: float32 [1024], P('hand'), may hold values from 0.1 to 1
- br_range: float32 [1024], P('hand'), may hold values from 0.001 to 1
- up_weight: bfloat16 [4, 256, 1024], P(None, 'leaf', 'hand'), may hold values from 0.29882812 to 1
- up_parent: int32 [3, 256], replicated, may hold values from 0 to 255
- board_cards: int32 [768, 5], P('leaf'), may hold values from 0 to 51, as said below
- hand_rank: int32 [768, 1024], P('leaf'), may hold values from 0 to 7461
- root_parent: int32 [768], P('leaf'), may hold values from 0 to 255
- br_actions: int32 [768], P('leaf'), may hold values from 1 to 8
- opp_actions: int32 [768, 8], P('leaf'), may hold values from 1 to 8
- leaf_kind: int32 [768, 8, 8], P('leaf'), may hold values from 0 to 1
- leaf_stake: int32 [768, 8, 8], P('leaf'), may hold values from 1 to 400
- opp_weight: bfloat16 [768, 8, 8, 1024], P('leaf', None, None, 'hand'), may hold values from 0.049804688 to 1
Outputs:
- level_values: float32 [4, 256, 1024], P(None, 'leaf', 'hand')
- root_value: float32 [1024], P('hand')
- best_value: float32 [], replicated
The draws below stay inside these ranges and needn't reach their ends.
Inputs may be any that keep to these rules, and one draw needn't show every extreme that they name: `board_cards`: five different cards for each subtree.
All inputs are finite; a program needn't handle non-finite values.
Results may differ from the reference program's by a relative error of at most 0.0003.
Values may be sent and summed in bfloat16 or wider, within the bound.
No kernel may reach another device: no remote copies, remote signals or barrier semaphores. Data moves between devices by JAX's collectives and lax.ppermute only.
A program may use at most 128 MiB of HBM per device.

```python
import math
import jax
import jax.numpy as jnp
import numpy as np
from jax import lax

HANDS = 1024
ACT = 8
UP = 4
UNODES = 256
SUBTREES = 768


def pick_cards(subkey):
    return jax.random.permutation(subkey, 52)[:5]


def draw_board_cards(key, part):
    subkeys = jax.random.split(jax.random.fold_in(key, 17), SUBTREES)
    return jax.vmap(pick_cards)(subkeys).astype(jnp.int32)


def set_ends(values, stream_key, least, high):
    shape = values.shape
    index_at = [jax.random.randint(jax.random.fold_in(stream_key, axis), (), 0, shape[axis]) for axis in range(len(shape))]
    values = values.at[tuple(index_at)].set(least)
    longest = shape.index(max(shape))
    index_at[longest] = (index_at[longest] + 1) % shape[longest]
    return values.at[tuple(index_at)].set(high)


def block_scale(key, extent, pieces, least, high):
    level, own = 1.0, jax.random.fold_in(key, 6)
    for dim, parts in pieces:
        steps = jnp.exp(jax.random.uniform(jax.random.fold_in(own, dim), (parts,), jnp.float32, least / len(pieces), high / len(pieces)))
        level = level * jnp.repeat(steps, extent[dim] // parts).reshape([-1 if axis == dim else 1 for axis in range(len(extent))])
    return level


def setup_inputs(seed: int = 0) -> dict:
    arg_keys = jax.random.split(jax.random.key(seed), 13)
    return {
        "opp_range": jnp.clip(jnp.exp(math.log(1.0) - 2.3025851 * jax.random.uniform(arg_keys[0], (HANDS,), jnp.float32) ** block_scale(arg_keys[0], (HANDS,), ((0, 4),), -0.2, 0.2)), 0.1, 1.0),
        "br_range": jnp.clip(jnp.exp(math.log(1.0) - 6.9077552 * jax.random.uniform(arg_keys[1], (HANDS,), jnp.float32) ** block_scale(arg_keys[1], (HANDS,), ((0, 4),), -0.2, 0.2)), 0.001, 1.0),
        "up_weight": jnp.clip(jnp.exp(math.log(1.0) - 1.2078867 * jax.random.uniform(arg_keys[2], (UP, UNODES, HANDS), jnp.float32) ** block_scale(arg_keys[2], (UP, UNODES, HANDS), ((1, 8), (2, 4)), -0.2, 0.2)), 0.29882812, 1.0).astype(jnp.bfloat16),
        "up_parent": set_ends(jax.random.randint(arg_keys[3], (UP - 1, UNODES), 0, UNODES), jax.random.fold_in(arg_keys[3], 1), 0, UNODES - 1).astype(jnp.int32),
        "board_cards": draw_board_cards(jax.random.fold_in(arg_keys[12], 71), 0),
        "hand_rank": set_ends(jax.random.randint(arg_keys[5], (SUBTREES, HANDS), 0, 7462), jax.random.fold_in(arg_keys[5], 1), 0, 7461).astype(jnp.int32),
        "root_parent": set_ends(jax.random.randint(arg_keys[6], (SUBTREES,), 0, UNODES), jax.random.fold_in(arg_keys[6], 1), 0, UNODES - 1).astype(jnp.int32),
        "br_actions": set_ends(jax.random.randint(arg_keys[7], (SUBTREES,), 1, ACT + 1), jax.random.fold_in(arg_keys[7], 1), 1, ACT).astype(jnp.int32),
        "opp_actions": set_ends(jax.random.randint(arg_keys[8], (SUBTREES, ACT), 1, ACT + 1), jax.random.fold_in(arg_keys[8], 1), 1, ACT).astype(jnp.int32),
        "leaf_kind": set_ends(jax.random.randint(arg_keys[9], (SUBTREES, ACT, ACT), 0, 2), jax.random.fold_in(arg_keys[9], 1), 0, 1).astype(jnp.int32),
        "leaf_stake": set_ends(jax.random.randint(arg_keys[10], (SUBTREES, ACT, ACT), 1, 401), jax.random.fold_in(arg_keys[10], 1), 1, 400).astype(jnp.int32),
        "opp_weight": jnp.clip(jnp.exp(math.log(1.0) - 2.9996462 * jax.random.uniform(arg_keys[11], (SUBTREES, ACT, ACT, HANDS), jnp.float32) ** block_scale(arg_keys[11], (SUBTREES, ACT, ACT, HANDS), ((0, 8), (3, 4)), -0.2, 0.2)), 0.049804688, 1.0).astype(jnp.bfloat16),
    }


PAYOFF_UNIT = 1.0 / 4096.0


def hand_cards(number):
    low_list = []
    high_list = []
    for low_card in range(52):
        for high_card in range(low_card + 1, 52):
            low_list.append(low_card)
            high_list.append(high_card)
    chosen = (np.arange(number) * 1326) // number
    return np.array(low_list, np.int32)[chosen], np.array(high_list, np.int32)[chosen]


def no_shared(low_rows, high_rows, low_cols, high_cols):
    apart_mask = (low_rows[:, None] != low_cols[None, :]) & (low_rows[:, None] != high_cols[None, :])
    apart_mask = apart_mask & (high_rows[:, None] != low_cols[None, :]) & (high_rows[:, None] != high_cols[None, :])
    return apart_mask.astype(jnp.float32)


def board_compat(board_cards, low_cols, high_cols):
    hits = (board_cards[:, :, None] == low_cols[None, None, :]) | (board_cards[:, :, None] == high_cols[None, None, :])
    return 1.0 - jnp.any(hits, axis=1).astype(jnp.float32)


def board_values(packed, noshare):
    root_row, compat_row, rank_row, opp_count, br_count, kind_rows, stake_rows, weight_rows = packed
    legal_mask = (jnp.arange(ACT)[None, :] < opp_count[:, None]).astype(jnp.float32)
    weighted = weight_rows.astype(jnp.float32) * legal_mask[:, :, None]
    probability = weighted / jnp.sum(weighted, axis=1, keepdims=True)
    leaf_reach = (root_row[None, None, :] * probability).astype(jnp.bfloat16).reshape(ACT * ACT, HANDS)
    reach_wide = leaf_reach.astype(jnp.float32)
    order_sign = jnp.sign(rank_row[None, :] - rank_row[:, None]).astype(jnp.float32) * noshare
    showdown = jnp.dot(reach_wide, order_sign, precision=lax.Precision.HIGHEST)
    folded = jnp.dot(reach_wide, noshare, precision=lax.Precision.HIGHEST)
    stake_scaled = stake_rows.reshape(-1).astype(jnp.float32) * PAYOFF_UNIT
    payoff = jnp.where(kind_rows.reshape(-1)[:, None] == 1, showdown, folded) * stake_scaled[:, None] * compat_row[None, :]
    per_node = jnp.sum(payoff.reshape(ACT, ACT, HANDS), axis=1)
    allowed = jnp.arange(ACT)[:, None] < br_count
    return jnp.max(jnp.where(allowed, per_node, -1e30), axis=0)


def reference(opp_range, br_range, up_weight, up_parent, board_cards, hand_rank, root_parent, br_actions, opp_actions, leaf_kind, leaf_stake, opp_weight):
    low_np, high_np = hand_cards(HANDS)
    low_all = jnp.asarray(low_np)
    high_all = jnp.asarray(high_np)
    compat = board_compat(board_cards, low_all, high_all)
    noshare = no_shared(low_all, high_all, low_all, high_all)
    reach_now = opp_range[None, :] * up_weight[0].astype(jnp.float32)
    for level_id in range(1, UP):
        reach_now = jnp.take(reach_now, up_parent[level_id - 1], axis=0) * up_weight[level_id].astype(jnp.float32)
    root_reach = jnp.take(reach_now, root_parent, axis=0) * compat

    def one_board(packed):
        return board_values(packed, noshare)

    sub_value = lax.map(one_board, (root_reach, compat, hand_rank, opp_actions, br_actions, leaf_kind, leaf_stake, opp_weight))
    level_sum = jax.ops.segment_sum(sub_value, root_parent, num_segments=UNODES)
    level_list = [level_sum]
    for level_id in range(UP - 1, 0, -1):
        level_sum = jax.ops.segment_sum(level_sum, up_parent[level_id - 1], num_segments=UNODES)
        level_list.insert(0, level_sum)
    level_values = jnp.stack(level_list)
    root_value = jnp.sum(level_values[0], axis=0) / UNODES
    best_value = jnp.sum(br_range * root_value) / jnp.sum(br_range)
    return level_values, root_value, best_value
```

```python
import functools

import jax
import jax.numpy as jnp
import numpy as np
from jax import lax
from jax.experimental import pallas as pl
from jax.experimental.pallas import tpu as pltpu
from jax.sharding import PartitionSpec as P

PAYOFF_UNIT = 1.0 / 4096.0
DIRECT_MAX = 8
PAD = 8
F32 = jnp.float32
BF16 = jnp.bfloat16
VMEM = pl.BlockSpec(memory_space=pltpu.VMEM)
SMEM = pl.BlockSpec(memory_space=pltpu.SMEM)


def hand_cards(number):
    low_list = []
    high_list = []
    for low_card in range(52):
        for high_card in range(low_card + 1, 52):
            low_list.append(low_card)
            high_list.append(high_card)
    chosen = np.arange(number) * 1326 // number
    return (np.array(low_list, np.int32)[chosen], np.array(high_list, np.int32)[chosen])


def no_shared(low_rows, high_rows, low_cols, high_cols):
    apart_mask = (low_rows[:, None] != low_cols[None, :]) & (
        low_rows[:, None] != high_cols[None, :]
    )
    return (
        apart_mask
        & (high_rows[:, None] != low_cols[None, :])
        & (high_rows[:, None] != high_cols[None, :])
    )


def board_compat(board_cards, low_cols, high_cols):
    hits = (board_cards[:, :, None] == low_cols[None, None, :]) | (
        board_cards[:, :, None] == high_cols[None, None, :]
    )
    return 1.0 - jnp.any(hits, axis=1).astype(F32)


def gather_pieces(x, axis, size):
    if size <= DIRECT_MAX:
        pieces = [x]
        for step in range(1, size):
            perm = [((i + step) % size, i) for i in range(size)]
            pieces.append(lax.ppermute(x, axis, perm))
        return pieces, True
    gathered = lax.all_gather(x, axis, axis=0)
    return [gathered[i] for i in range(size)], False


def root_kernel(levels, nodes, chunks, boards, anc_ref, opp_ref, compat_ref, br_ref, *refs):
    pieces, outs, wide = refs[: -chunks - 1], refs[-chunks - 1 : -1], refs[-1]
    total = nodes * len(pieces)
    for p, piece in enumerate(pieces):
        for k in range(levels):
            wide[k * total + p * nodes : k * total + (p + 1) * nodes, :] = piece[
                k * nodes : (k + 1) * nodes, :
            ]
    count = anc_ref.shape[0]
    lanes = lax.broadcasted_iota(jnp.int32, (count, total), 1)
    reach = jnp.broadcast_to(opp_ref[...], (count, opp_ref.shape[1]))
    for k in range(levels):
        pick = (lanes == anc_ref[:, k : k + 1]).astype(F32).astype(BF16)
        reach = reach * jnp.dot(
            pick, wide[k * total : (k + 1) * total, :], preferred_element_type=F32
        )
    reach = reach * compat_ref[...]
    for j in range(chunks):
        outs[j][0:boards, :] = reach[j * boards : (j + 1) * boards, :]
        outs[j][boards : boards + PAD, :] = jnp.broadcast_to(
            br_ref[...], (PAD, opp_ref.shape[1])
        )


def main_kernel(chunks, boards, actions, info_ref, count_ref, rank_ref, compat_ref, ns_ref, *refs):
    roots, ys = refs[:chunks], refs[chunks : 2 * chunks]
    outs = refs[2 * chunks : 3 * chunks]
    neg, xs, xf, rank_f, fold, sub = refs[3 * chunks :]
    width = roots[0].shape[1]
    hands = width * chunks
    rank_f[...] = rank_ref[...].astype(F32)
    neg[...] = -ns_ref[...]

    def prepare(i, carry):
        for j in range(chunks):
            x = ys[j][i] * roots[j][pl.ds(i, 1), :]
            high = x.astype(BF16).astype(F32)
            low = x - high
            cols = slice(j * width, (j + 1) * width)
            xs[i, :, cols] = jnp.concatenate([high[:actions], low[:actions]], 0).astype(BF16)
            xf[i, :, cols] = jnp.concatenate([high[actions:], low[actions:]], 0).astype(BF16)
        return carry

    lax.fori_loop(0, boards, prepare, 0)
    left = xf[...].reshape(boards * 2 * actions, hands)
    for j in range(chunks):
        cols = slice(j * width, (j + 1) * width)
        both = jnp.dot(left, ns_ref[:, cols], preferred_element_type=F32)
        both = both.reshape(boards, 2 * actions, width)
        fold[:, :, cols] = both[:, :actions] + both[:, actions:]

    def one_board(i, carry):
        rank = rank_f[pl.ds(i, 1), :]
        coarse = jnp.floor(rank * (1.0 / 64.0)) * 64.0
        fine = rank - coarse
        allowed = lax.broadcasted_iota(jnp.int32, (actions, width), 0) < count_ref[i]
        columns = []
        for b in range(hands // 128):
            part = slice(b * 128, (b + 1) * 128)
            columns.append(
                tuple(
                    jnp.broadcast_to(v[:, part], (128, 128)).T.astype(BF16) for v in (coarse, fine)
                )
            )
        for j in range(chunks):
            acc = None
            cols = slice(j * width, (j + 1) * width)
            for r in range(hands // 256):
                halves = []
                for s in range(2):
                    o_high, o_low = columns[r * 2 + s]
                    rows = slice(r * 256 + s * 128, r * 256 + (s + 1) * 128)
                    tiles = []
                    for c in range(width // 128):
                        part = slice(j * width + c * 128, j * width + (c + 1) * 128)
                        h_high = jnp.broadcast_to(coarse[:, part], (128, 128)).astype(BF16)
                        h_low = jnp.broadcast_to(fine[:, part], (128, 128)).astype(BF16)
                        gap = (h_high - o_high) + (h_low - o_low)
                        tiles.append(
                            jnp.maximum(jnp.minimum(gap, ns_ref[rows, part]), neg[rows, part])
                        )
                    halves.append(jnp.concatenate(tiles, 1))
                block = jnp.concatenate(halves, 0)
                term = jnp.dot(
                    xs[i, :, r * 256 : (r + 1) * 256], block, preferred_element_type=F32
                )
                acc = term if acc is None else acc + term
            node = acc[:actions] + acc[actions:] + fold[i, :, cols]
            best = jnp.max(jnp.where(allowed, node, -1e30), axis=0, keepdims=True)
            sub[pl.ds(i, 1), cols] = best * compat_ref[pl.ds(i, 1), cols]
        return carry

    lax.fori_loop(0, boards, one_board, 0)
    weighted = jnp.zeros((1, 1), F32)
    for j in range(chunks):
        cols = slice(j * width, (j + 1) * width)
        weighted += jnp.sum(sub[:, cols] * roots[j][boards : boards + 1, :], keepdims=True)
    share = jnp.sum(roots[0][boards : boards + 1, :], keepdims=True)
    lanes = lax.broadcasted_iota(jnp.int32, (PAD, width), 1)
    rows = lax.broadcasted_iota(jnp.int32, (PAD, width), 0)
    mine = lanes == info_ref[0]
    first = info_ref[1] == 0
    tail = jnp.where(mine & (rows == 0), weighted, 0.0)
    tail = tail + jnp.where(mine & (rows == 1) & first, share, 0.0)
    for j in range(chunks):
        outs[j][0:boards, :] = sub[:, j * width : (j + 1) * width]
        outs[j][boards : boards + PAD, :] = tail


def tail_kernel(levels, nodes, node_total, chunks, boards, start_ref, anc_ref, *refs):
    pieces, (level_ref, root_ref, best_ref) = refs[:-3], refs[-3:]
    rows = chunks * (boards + PAD)
    ids = lax.broadcasted_iota(jnp.int32, (nodes, rows), 0) + start_ref[0]
    acc = None
    total = None
    extra = None
    for p, piece in enumerate(pieces):
        pick = jnp.concatenate(
            [
                (ids == anc_ref[k : k + 1, p * rows : (p + 1) * rows]).astype(F32)
                for k in range(levels)
            ],
            0,
        ).astype(BF16)
        value = piece[...]
        for _ in range(3):
            part = value.astype(BF16)
            term = jnp.dot(pick, part, preferred_element_type=F32)
            acc = term if acc is None else acc + term
            value = value - part.astype(F32)
        for j in range(chunks):
            at = j * (boards + PAD)
            one = piece[at : at + boards, :]
            two = piece[at + boards : at + boards + PAD, :]
            total = one if total is None else total + one
            extra = two if extra is None else extra + two
    level_ref[...] = acc
    root_ref[...] = jnp.sum(total, axis=0, keepdims=True) * (1.0 / node_total)
    weighted = jnp.sum(extra[0:1, :], axis=1, keepdims=True) * (1.0 / node_total)
    best_ref[...] = weighted / jnp.sum(extra[1:2, :], axis=1, keepdims=True)


def local(
    opp_range,
    br_range,
    up_weight,
    up_parent,
    board_cards,
    hand_rank,
    root_parent,
    br_actions,
    opp_actions,
    leaf_kind,
    leaf_stake,
    opp_weight,
):
    levels, nodes, width = up_weight.shape
    boards_dev = board_cards.shape[0]
    actions = opp_actions.shape[1]
    hands = hand_rank.shape[1]
    leaf_size = lax.axis_size("leaf")
    chunks = lax.axis_size("hand")
    boards = boards_dev // chunks
    node_total = nodes * leaf_size
    leaf = lax.axis_index("leaf")
    hand = lax.axis_index("hand")
    low_np, high_np = hand_cards(hands)
    low_all = jnp.asarray(low_np)
    high_all = jnp.asarray(high_np)

    lane_pad = ((0, 0), (0, width - boards_dev))
    parent_rows = jnp.stack([root_parent // 128, root_parent % 128]).astype(BF16)
    parent_rows = jnp.pad(parent_rows, ((0, 14), lane_pad[1]))
    payload = jnp.concatenate([up_weight.reshape(levels * nodes, width), parent_rows], 0)
    up_pieces, relative = gather_pieces(payload, "leaf", leaf_size)

    def boards_of(x, j):
        return lax.dynamic_slice_in_dim(x, ((hand + j) % chunks) * boards, boards, 0)

    y_list = []
    for j in range(chunks):
        weight = boards_of(opp_weight, j).astype(F32)
        legal = (
            jnp.arange(actions)[None, None, :] < boards_of(opp_actions, j)[:, :, None]
        ).astype(F32)
        stake = boards_of(leaf_stake, j).astype(F32) * PAYOFF_UNIT * legal
        shows = boards_of(leaf_kind, j) == 1
        scale = 1.0 / jnp.sum(weight * legal[..., None], axis=2)
        show = jnp.sum(weight * jnp.where(shows, stake, 0.0)[..., None], axis=2) * scale
        fold = jnp.sum(weight * jnp.where(shows, 0.0, stake)[..., None], axis=2) * scale
        y_list.append(jnp.concatenate([show, fold], 1))
    y_list = exchange(y_list, chunks, 1)

    def rolled(x):
        return jnp.concatenate([boards_of(x, j) for j in range(chunks)], 0)

    low_mine = lax.dynamic_slice_in_dim(low_all, hand * width, width)
    high_mine = lax.dynamic_slice_in_dim(high_all, hand * width, width)
    compat_mine = board_compat(rolled(board_cards), low_mine, high_mine)

    def ancestors(at):
        chain = [at]
        for k in range(levels - 1, 0, -1):
            at = jnp.take(up_parent[k - 1], at, mode="clip")
            chain.insert(0, at)
        return chain

    mine = jnp.stack(ancestors(rolled(root_parent)), 1)
    if relative:
        mine = (mine - leaf * nodes) % node_total
    message = jax.ShapeDtypeStruct((boards + PAD, width), F32)
    root_list = pl.pallas_call(
        functools.partial(root_kernel, levels, nodes, chunks, boards),
        out_shape=[message] * chunks,
        in_specs=[VMEM] * (4 + len(up_pieces)),
        out_specs=[VMEM] * chunks,
        scratch_shapes=[pltpu.VMEM((levels * node_total, width), BF16)],
        compiler_params=pltpu.CompilerParams(vmem_limit_bytes=32 << 20),
        cost_estimate=pl.CostEstimate(
            flops=2 * levels * boards_dev * node_total * width,
            bytes_accessed=2 * levels * node_total * width,
            transcendentals=0,
        ),
        name="root_reach",
    )(mine, opp_range[None, :], compat_mine, br_range[None, :], *up_pieces)
    root_list = exchange(root_list, chunks, 1)

    def hands_of(x):
        return jnp.concatenate(
            [
                lax.dynamic_slice_in_dim(x, ((hand - j) % chunks) * width, width, x.ndim - 1)
                for j in range(chunks)
            ],
            x.ndim - 1,
        )

    low_rel = hands_of(low_all)
    high_rel = hands_of(high_all)
    apart = no_shared(low_rel, high_rel, low_rel, high_rel).astype(BF16)
    rank = hands_of(boards_of(hand_rank, 0))
    compat_all = board_compat(boards_of(board_cards, 0), low_rel, high_rel)
    info = jnp.stack([leaf * chunks + hand, leaf])
    sub_list = pl.pallas_call(
        functools.partial(main_kernel, chunks, boards, actions),
        out_shape=[message] * chunks,
        in_specs=[SMEM, SMEM] + [VMEM] * (3 + 2 * chunks),
        out_specs=[VMEM] * chunks,
        scratch_shapes=[
            pltpu.VMEM((hands, hands), BF16),
            pltpu.VMEM((boards, 2 * actions, hands), BF16),
            pltpu.VMEM((boards, 2 * actions, hands), BF16),
            pltpu.VMEM((boards, hands), F32),
            pltpu.VMEM((boards, actions, hands), F32),
            pltpu.VMEM((boards, hands), F32),
        ],
        compiler_params=pltpu.CompilerParams(vmem_limit_bytes=48 << 20),
        cost_estimate=pl.CostEstimate(
            flops=2 * boards * 2 * actions * hands * hands,
            bytes_accessed=4 * hands * hands,
            transcendentals=0,
        ),
        name="best_response",
    )(info, boards_of(br_actions, 0), rank, compat_all, apart, *root_list, *y_list)
    sub_list = exchange(sub_list, chunks, -1)

    halves = jnp.stack([piece[levels * nodes : levels * nodes + 2, :boards_dev] for piece in up_pieces])
    parents = halves[:, 0].astype(jnp.int32) * 128 + halves[:, 1].astype(jnp.int32)
    parents = parents.reshape(leaf_size, chunks, boards)
    parents = jnp.concatenate(
        [
            lax.dynamic_slice_in_dim(parents, (hand + j) % chunks, 1, 1)
            for j in range(chunks)
        ],
        1,
    )
    chain = jnp.stack(ancestors(parents.reshape(-1)))
    chain = chain.reshape(levels, leaf_size, chunks, boards)
    chain = jnp.pad(chain, ((0, 0), (0, 0), (0, 0), (0, PAD)), constant_values=-1)
    chain = chain.reshape(levels, leaf_size * chunks * (boards + PAD))
    sub_pieces, _ = gather_pieces(jnp.concatenate(sub_list, 0), "leaf", leaf_size)
    level_flat, root_value, best_value = pl.pallas_call(
        functools.partial(tail_kernel, levels, nodes, node_total, chunks, boards),
        out_shape=[
            jax.ShapeDtypeStruct((levels * nodes, width), F32),
            jax.ShapeDtypeStruct((1, width), F32),
            jax.ShapeDtypeStruct((1, 1), F32),
        ],
        in_specs=[SMEM] + [VMEM] * (1 + len(sub_pieces)),
        out_specs=[VMEM] * 3,
        compiler_params=pltpu.CompilerParams(vmem_limit_bytes=32 << 20),
        name="level_sums",
    )((leaf * nodes)[None], chain, *sub_pieces)
    return (level_flat.reshape(levels, nodes, width), root_value[0], best_value[0, 0])


def exchange(blocks, size, way):
    moved = [blocks[0]]
    for step in range(1, size):
        perm = [(i, (i + way * step) % size) for i in range(size)]
        moved.append(lax.ppermute(blocks[step], "hand", perm))
    return moved


def solution(mesh):
    in_specs = (
        P("hand"),
        P("hand"),
        P(None, "leaf", "hand"),
        P(),
        P("leaf", None),
        P("leaf", None),
        P("leaf"),
        P("leaf"),
        P("leaf", None),
        P("leaf", None, None),
        P("leaf", None, None),
        P("leaf", None, None, "hand"),
    )
    out_specs = (P(None, "leaf", "hand"), P("hand"), P())
    return jax.shard_map(local, mesh=mesh, in_specs=in_specs, out_specs=out_specs, check_vma=False)
```

```python
import functools

import jax
import jax.numpy as jnp
import numpy as np
from jax import lax
from jax.experimental import pallas as pl
from jax.experimental.pallas import tpu as pltpu
from jax.sharding import PartitionSpec as P

PAYOFF_UNIT = 1.0 / 4096.0
DIRECT_MAX = 8
PAD = 8
F32 = jnp.float32
BF16 = jnp.bfloat16
VMEM = pl.BlockSpec(memory_space=pltpu.VMEM)
SMEM = pl.BlockSpec(memory_space=pltpu.SMEM)


def hand_cards(number):
    low_list = []
    high_list = []
    for low_card in range(52):
        for high_card in range(low_card + 1, 52):
            low_list.append(low_card)
            high_list.append(high_card)
    chosen = np.arange(number) * 1326 // number
    return (np.array(low_list, np.int32)[chosen], np.array(high_list, np.int32)[chosen])


def no_shared(low_rows, high_rows, low_cols, high_cols):
    apart_mask = (low_rows[:, None] != low_cols[None, :]) & (
        low_rows[:, None] != high_cols[None, :]
    )
    return (
        apart_mask
        & (high_rows[:, None] != low_cols[None, :])
        & (high_rows[:, None] != high_cols[None, :])
    )


def board_compat(board_cards, low_cols, high_cols):
    hits = (board_cards[:, :, None] == low_cols[None, None, :]) | (
        board_cards[:, :, None] == high_cols[None, None, :]
    )
    return 1.0 - jnp.any(hits, axis=1).astype(F32)


def gather_pieces(x, axis, size):
    if size <= DIRECT_MAX:
        pieces = [x]
        for step in range(1, size):
            perm = [((i + step) % size, i) for i in range(size)]
            pieces.append(lax.ppermute(x, axis, perm))
        return pieces, True
    gathered = lax.all_gather(x, axis, axis=0)
    return [gathered[i] for i in range(size)], False


def root_kernel(levels, nodes, chunks, boards, relative, info_ref, parent_ref, up_ref, opp_ref, compat_ref, br_ref, *refs):
    count = len(refs) - chunks - 3
    pieces, outs = refs[:count], refs[count : count + chunks]
    chain_ref, wide, reach_s = refs[count + chunks :]
    total = nodes * count
    for p, piece in enumerate(pieces):
        owner = lax.rem(info_ref[0] + p, count) if relative else p
        for k in range(levels):
            at = pl.multiple_of(k * total + owner * nodes, nodes)
            wide[pl.ds(at, nodes), :] = piece[k * nodes : (k + 1) * nodes, :]
    lanes = parent_ref.shape[1]
    width = opp_ref.shape[1]
    ids = lax.broadcasted_iota(jnp.int32, (total, lanes), 0).astype(F32)
    above = parent_ref[...].astype(F32)
    rows = [None] * levels
    reach = None
    for k in range(levels - 1, -1, -1):
        rows[k] = above
        pick = (ids == above).astype(F32).astype(BF16)
        gain = lax.dot_general(
            pick,
            wide[k * total : (k + 1) * total, :],
            (((0,), (0,)), ((), ())),
            preferred_element_type=F32,
        )
        reach_s[k * lanes : (k + 1) * lanes, :] = gain
        if k > 0:
            found = jnp.dot(up_ref[...], pick, preferred_element_type=F32)
            above = found[k - 1 : k, :] + found[PAD + k - 1 : PAD + k, :]
    reach = jnp.broadcast_to(opp_ref[...], (lanes, width))
    for k in range(levels):
        reach = reach * reach_s[k * lanes : (k + 1) * lanes, :]
    boards_dev = chunks * boards
    reach_s[0:boards_dev, :] = reach[:boards_dev] * compat_ref[...]
    for j in range(chunks):
        at = pl.multiple_of(lax.rem(info_ref[1] + j, chunks) * boards, 8)
        outs[j][0:boards, :] = reach_s[pl.ds(at, boards), :]
        outs[j][boards : boards + PAD, :] = jnp.broadcast_to(br_ref[...], (PAD, width))
    zero = jnp.zeros((1, lanes), F32)
    chain = jnp.concatenate([zero, zero] + rows + [zero] * (PAD - 2 - levels), 0)
    chain = pltpu.roll(chain, lax.rem(lanes - info_ref[1] * boards, lanes), 1)
    keep = lax.broadcasted_iota(jnp.int32, (PAD, lanes), 1) < boards
    chain_ref[...] = jnp.where(keep, chain, 0.0)


def main_kernel(chunks, boards, actions, info_ref, count_ref, chain_ref, rank_ref, compat_ref, ns_ref, *refs):
    roots, ys = refs[:chunks], refs[chunks : 2 * chunks]
    outs = refs[2 * chunks : 3 * chunks]
    neg, xs, xf, rank_f, fold, sub = refs[3 * chunks :]
    width = roots[0].shape[1]
    hands = width * chunks
    rank_f[...] = rank_ref[...].astype(F32)
    neg[...] = -ns_ref[...]

    def prepare(i, carry):
        for j in range(chunks):
            x = ys[j][i] * roots[j][pl.ds(i, 1), :]
            high = x.astype(BF16).astype(F32)
            low = x - high
            cols = slice(j * width, (j + 1) * width)
            xs[i, :, cols] = jnp.concatenate([high[:actions], low[:actions]], 0).astype(BF16)
            xf[i, :, cols] = jnp.concatenate([high[actions:], low[actions:]], 0).astype(BF16)
        return carry

    lax.fori_loop(0, boards, prepare, 0)
    left = xf[...].reshape(boards * 2 * actions, hands)
    for j in range(chunks):
        cols = slice(j * width, (j + 1) * width)
        both = jnp.dot(left, ns_ref[:, cols], preferred_element_type=F32)
        both = both.reshape(boards, 2 * actions, width)
        fold[:, :, cols] = both[:, :actions] + both[:, actions:]

    def one_board(i, carry):
        rank = rank_f[pl.ds(i, 1), :]
        coarse = jnp.floor(rank * (1.0 / 64.0)) * 64.0
        fine = rank - coarse
        allowed = lax.broadcasted_iota(jnp.int32, (actions, width), 0) < count_ref[i]
        columns = []
        for b in range(hands // 128):
            part = slice(b * 128, (b + 1) * 128)
            columns.append(
                tuple(
                    jnp.broadcast_to(v[:, part], (128, 128)).T.astype(BF16) for v in (coarse, fine)
                )
            )
        for j in range(chunks):
            acc = None
            cols = slice(j * width, (j + 1) * width)
            for r in range(hands // 256):
                halves = []
                for s in range(2):
                    o_high, o_low = columns[r * 2 + s]
                    rows = slice(r * 256 + s * 128, r * 256 + (s + 1) * 128)
                    tiles = []
                    for c in range(width // 128):
                        part = slice(j * width + c * 128, j * width + (c + 1) * 128)
                        h_high = jnp.broadcast_to(coarse[:, part], (128, 128)).astype(BF16)
                        h_low = jnp.broadcast_to(fine[:, part], (128, 128)).astype(BF16)
                        gap = (h_high - o_high) + (h_low - o_low)
                        tiles.append(
                            jnp.maximum(jnp.minimum(gap, ns_ref[rows, part]), neg[rows, part])
                        )
                    halves.append(jnp.concatenate(tiles, 1))
                block = jnp.concatenate(halves, 0)
                term = jnp.dot(
                    xs[i, :, r * 256 : (r + 1) * 256], block, preferred_element_type=F32
                )
                acc = term if acc is None else acc + term
            node = acc[:actions] + acc[actions:] + fold[i, :, cols]
            best = jnp.max(jnp.where(allowed, node, -1e30), axis=0, keepdims=True)
            sub[pl.ds(i, 1), cols] = best * compat_ref[pl.ds(i, 1), cols]
        return carry

    lax.fori_loop(0, boards, one_board, 0)
    weighted = jnp.zeros((1, 1), F32)
    for j in range(chunks):
        cols = slice(j * width, (j + 1) * width)
        weighted += jnp.sum(sub[:, cols] * roots[j][boards : boards + 1, :], keepdims=True)
    share = jnp.sum(roots[0][boards : boards + 1, :], keepdims=True)
    lanes = lax.broadcasted_iota(jnp.int32, (PAD, width), 1)
    rows = lax.broadcasted_iota(jnp.int32, (PAD, width), 0)
    mine = lanes == info_ref[0] * chunks + info_ref[1]
    first = info_ref[0] == 0
    tail = jnp.where(mine & (rows == 0), weighted, 0.0)
    tail = tail + jnp.where(mine & (rows == 1) & first, share, 0.0)
    for j in range(chunks):
        outs[j][0:boards, :] = sub[:, j * width : (j + 1) * width]
        moved = pltpu.roll(chain_ref[...], boards * j, 1) if j else chain_ref[...]
        blank = jnp.zeros((PAD, width - moved.shape[1]), F32)
        outs[j][boards : boards + PAD, :] = tail + jnp.concatenate([moved, blank], 1)


def tail_kernel(levels, nodes, node_total, start_ref, *refs):
    pieces, (level_ref, root_ref, best_ref) = refs[:-3], refs[-3:]
    rows = pieces[0].shape[0] - PAD
    ids = lax.broadcasted_iota(jnp.int32, (nodes, rows), 0) + start_ref[0] * nodes
    ids = ids.astype(F32)
    acc = None
    total = None
    extra = None
    for piece in pieces:
        tags = piece[rows : rows + PAD, :]
        pick = jnp.concatenate(
            [(ids == tags[2 + k : 3 + k, :rows]).astype(F32) for k in range(levels)], 0
        ).astype(BF16)
        value = piece[0:rows, :]
        total = value if total is None else total + value
        extra = tags if extra is None else extra + tags
        for _ in range(3):
            part = value.astype(BF16)
            term = jnp.dot(pick, part, preferred_element_type=F32)
            acc = term if acc is None else acc + term
            value = value - part.astype(F32)
    level_ref[...] = acc
    root_ref[...] = jnp.sum(total, axis=0, keepdims=True) * (1.0 / node_total)
    weighted = jnp.sum(extra[0:1, :], axis=1, keepdims=True) * (1.0 / node_total)
    best_ref[...] = weighted / jnp.sum(extra[1:2, :], axis=1, keepdims=True)


def local(
    opp_range,
    br_range,
    up_weight,
    up_parent,
    board_cards,
    hand_rank,
    root_parent,
    br_actions,
    opp_actions,
    leaf_kind,
    leaf_stake,
    opp_weight,
):
    levels, nodes, width = up_weight.shape
    boards_dev = board_cards.shape[0]
    actions = opp_actions.shape[1]
    hands = hand_rank.shape[1]
    leaf_size = lax.axis_size("leaf")
    chunks = lax.axis_size("hand")
    boards = boards_dev // chunks
    node_total = nodes * leaf_size
    leaf = lax.axis_index("leaf")
    hand = lax.axis_index("hand")
    low_np, high_np = hand_cards(hands)
    low_all = jnp.asarray(low_np)
    high_all = jnp.asarray(high_np)

    up_pieces, relative = gather_pieces(
        up_weight.reshape(levels * nodes, width), "leaf", leaf_size
    )

    def boards_of(x, j):
        return lax.dynamic_slice_in_dim(x, ((hand + j) % chunks) * boards, boards, 0)

    y_list = []
    for j in range(chunks):
        weight = boards_of(opp_weight, j).astype(F32)
        legal = (
            jnp.arange(actions)[None, None, :] < boards_of(opp_actions, j)[:, :, None]
        ).astype(F32)
        stake = boards_of(leaf_stake, j).astype(F32) * PAYOFF_UNIT * legal
        shows = boards_of(leaf_kind, j) == 1
        scale = 1.0 / jnp.sum(weight * legal[..., None], axis=2)
        show = jnp.sum(weight * jnp.where(shows, stake, 0.0)[..., None], axis=2) * scale
        fold = jnp.sum(weight * jnp.where(shows, 0.0, stake)[..., None], axis=2) * scale
        y_list.append(jnp.concatenate([show, fold], 1))
    y_list = exchange(y_list, chunks, 1)

    low_mine = lax.dynamic_slice_in_dim(low_all, hand * width, width)
    high_mine = lax.dynamic_slice_in_dim(high_all, hand * width, width)
    compat_mine = board_compat(board_cards, low_mine, high_mine)
    parent_row = jnp.pad(root_parent, (0, -boards_dev % 128), constant_values=-1)[None, :]
    coarse = up_parent // 128 * 128
    fill = ((0, PAD - levels + 1), (0, 0))
    up_rows = jnp.concatenate([jnp.pad(coarse, fill), jnp.pad(up_parent - coarse, fill)], 0)
    info = jnp.stack([leaf, hand])
    message = jax.ShapeDtypeStruct((boards + PAD, width), F32)
    lanes = parent_row.shape[1]
    *root_list, chain = pl.pallas_call(
        functools.partial(root_kernel, levels, nodes, chunks, boards, relative),
        out_shape=[message] * chunks + [jax.ShapeDtypeStruct((PAD, lanes), F32)],
        in_specs=[SMEM] + [VMEM] * (5 + len(up_pieces)),
        out_specs=[VMEM] * (chunks + 1),
        scratch_shapes=[
            pltpu.VMEM((levels * node_total, width), BF16),
            pltpu.VMEM((levels * lanes, width), F32),
        ],
        compiler_params=pltpu.CompilerParams(vmem_limit_bytes=32 << 20),
        cost_estimate=pl.CostEstimate(
            flops=2 * levels * boards_dev * node_total * width,
            bytes_accessed=2 * levels * node_total * width,
            transcendentals=0,
        ),
        name="root_reach",
    )(info, parent_row, up_rows.astype(BF16), opp_range[None, :], compat_mine, br_range[None, :], *up_pieces)
    root_list = exchange(root_list, chunks, 1)

    def hands_of(x):
        return jnp.concatenate(
            [
                lax.dynamic_slice_in_dim(x, ((hand - j) % chunks) * width, width, x.ndim - 1)
                for j in range(chunks)
            ],
            x.ndim - 1,
        )

    low_rel = hands_of(low_all)
    high_rel = hands_of(high_all)
    apart = no_shared(low_rel, high_rel, low_rel, high_rel).astype(BF16)
    rank = hands_of(boards_of(hand_rank, 0))
    compat_all = board_compat(boards_of(board_cards, 0), low_rel, high_rel)
    sub_list = pl.pallas_call(
        functools.partial(main_kernel, chunks, boards, actions),
        out_shape=[message] * chunks,
        in_specs=[SMEM, SMEM] + [VMEM] * (4 + 2 * chunks),
        out_specs=[VMEM] * chunks,
        scratch_shapes=[
            pltpu.VMEM((hands, hands), BF16),
            pltpu.VMEM((boards, 2 * actions, hands), BF16),
            pltpu.VMEM((boards, 2 * actions, hands), BF16),
            pltpu.VMEM((boards, hands), F32),
            pltpu.VMEM((boards, actions, hands), F32),
            pltpu.VMEM((boards, hands), F32),
        ],
        compiler_params=pltpu.CompilerParams(vmem_limit_bytes=48 << 20),
        cost_estimate=pl.CostEstimate(
            flops=2 * boards * 2 * actions * hands * hands,
            bytes_accessed=4 * hands * hands,
            transcendentals=0,
        ),
        name="best_response",
    )(info, boards_of(br_actions, 0), chain, rank, compat_all, apart, *root_list, *y_list)
    sub_list = exchange(sub_list, chunks, -1)

    packed = [x[:boards] for x in sub_list] + [sum(x[boards:] for x in sub_list)]
    sub_pieces, _ = gather_pieces(jnp.concatenate(packed, 0), "leaf", leaf_size)
    level_flat, root_value, best_value = pl.pallas_call(
        functools.partial(tail_kernel, levels, nodes, node_total),
        out_shape=[
            jax.ShapeDtypeStruct((levels * nodes, width), F32),
            jax.ShapeDtypeStruct((1, width), F32),
            jax.ShapeDtypeStruct((1, 1), F32),
        ],
        in_specs=[SMEM] + [VMEM] * len(sub_pieces),
        out_specs=[VMEM] * 3,
        compiler_params=pltpu.CompilerParams(vmem_limit_bytes=32 << 20),
        name="level_sums",
    )(info, *sub_pieces)
    return (level_flat.reshape(levels, nodes, width), root_value[0], best_value[0, 0])


def exchange(blocks, size, way):
    moved = [blocks[0]]
    for step in range(1, size):
        perm = [(i, (i + way * step) % size) for i in range(size)]
        moved.append(lax.ppermute(blocks[step], "hand", perm))
    return moved


def solution(mesh):
    in_specs = (
        P("hand"),
        P("hand"),
        P(None, "leaf", "hand"),
        P(),
        P("leaf", None),
        P("leaf", None),
        P("leaf"),
        P("leaf"),
        P("leaf", None),
        P("leaf", None, None),
        P("leaf", None, None),
        P("leaf", None, None, "hand"),
    )
    out_specs = (P(None, "leaf", "hand"), P("hand"), P())
    return jax.shard_map(local, mesh=mesh, in_specs=in_specs, out_specs=out_specs, check_vma=False)
```
